128 devices in a mesh: row: 8 (over z, y_lo), col: 16 (over x, y_hi, core).
Axes of the slice: x: 4, y: 4 (y_hi: 2, y_lo: 2; y = y_hi * 2 + y_lo), z: 4, core: 2. Of those that a mesh axis runs over, the one named last changes fastest.
Arguments:
- factor_panel: float32 [16384, 512], P(('row', 'col')), may hold values from -0.6 to 0.6
- pivot_inverse: float32 [512, 512], replicated, may hold values from -3 to 3
- ancestor_inverse: float32 [16384, 16384], P('row', 'col'), may hold values from -0.046875 to 0.046875
- diag_inverse: float32 [512, 512], replicated, may hold values from -6 to 6
- block_map: int32 [128], replicated, may hold values from 0 to 127, as said below
Outputs:
- offdiag_block: float32 [16384, 512], P(('row', 'col'))
- diag_block: float32 [512, 512], replicated
The draws below stay inside these ranges and needn't reach their ends.
Inputs may be any that keep to these rules, and one draw needn't show every extreme that they name: block_map is a permutation of the blocks that maps every aligned group of 16 blocks onto itself.
All inputs are finite; a program needn't handle non-finite values.
Results may differ from the reference program's by a relative error of at most 0.000071.
Values sent between devices are 32-bit elements; how exact they have to be, the bound alone decides.
No kernel may reach another device: no remote copies, remote signals or barrier semaphores. Data moves between devices by JAX's collectives and lax.ppermute only.
A program may use at most 128 MiB of HBM per device.

```python
import jax
import jax.numpy as jnp
from jax import lax

A = 16384
S = 512
BLOCK = 128
NB = 128
GB = 16


def draw_pivot_inverse(key, part):
    first_key, second_key = jax.random.split(key)
    leading = jax.random.uniform(first_key, (S,), jnp.float32, 0.7, 1.3)
    spread = jax.random.normal(second_key, (S, S), jnp.float32) * (0.6 / S ** 0.5)
    return jnp.diag(leading) + spread


def draw_block_map(key, part):
    positions = jnp.arange(NB, dtype=jnp.int32)
    jitter = jax.random.randint(key, (NB,), 0, 4096, dtype=jnp.int32)
    scores = positions // GB * 4194304 + jitter * 1024 + positions
    return jnp.argsort(scores, stable=True).astype(jnp.int32)


def steps_of(rng, dims, cuts, low, largest):
    def one(axis_at, parts):
        heights = jax.random.uniform(jax.random.fold_in(jax.random.fold_in(rng, 6), axis_at), (parts,), jnp.float32, low / len(cuts), largest / len(cuts))
        return jnp.repeat(jnp.exp(heights), dims[axis_at] // parts).reshape((-1,) + (1,) * (len(dims) - axis_at - 1))

    factor_of = one(*cuts[0])
    for cut in cuts[1:]:
        factor_of = factor_of * one(*cut)
    return factor_of


def normal_values(key, dims, scale, bound, pieces=(), kind=jnp.bfloat16):
    array = jax.random.normal(key, dims, jnp.float32) * scale
    if len(pieces) > 0:
        array = steps_of(key, dims, pieces, -0.22, 0.18) * array
    return jnp.clip(array, min=-bound, max=bound).astype(kind)


def setup_inputs(seed: int = 0) -> dict:
    keys = jax.random.split(jax.random.key(seed), 6)
    return {
        "factor_panel": normal_values(keys[0], (A, S), 0.088, 0.6, ((0, 128),), jnp.float32),
        "pivot_inverse": draw_pivot_inverse(jax.random.fold_in(keys[5], 71), 0),
        "ancestor_inverse": normal_values(keys[2], (A, A), A ** -0.5, 0.046875, ((0, 8), (1, 16)), jnp.float32),
        "diag_inverse": normal_values(keys[3], (S, S), 1.0, 6.0, (), jnp.float32),
        "block_map": draw_block_map(jax.random.fold_in(keys[5], 71), 0),
    }


def reference(factor_panel, pivot_inverse, ancestor_inverse, diag_inverse, block_map):
    highest = lax.Precision.HIGHEST
    normed = jnp.dot(factor_panel, pivot_inverse, precision=highest, preferred_element_type=jnp.float32)
    positions = jnp.arange(NB, dtype=jnp.int32)
    source = jnp.sum(jnp.where(block_map[None, :] == positions[:, None], positions[None, :], 0), axis=1).astype(jnp.int32)
    blocks_all = normed.reshape(NB, BLOCK, S)
    ordered = jnp.take(blocks_all, source, axis=0).reshape(A, S)
    offdiag_block = -jnp.dot(ancestor_inverse, ordered, precision=highest, preferred_element_type=jnp.float32)
    product = lax.dot_general(ordered, offdiag_block, (((0,), (0,)), ((), ())), precision=highest, preferred_element_type=jnp.float32)
    diag_block = diag_inverse - product
    return offdiag_block, diag_block
```

```python
import jax
import jax.numpy as jnp
from jax import lax
from jax.sharding import Mesh, PartitionSpec as P

BLOCK = 128
ROW = ("z", "yl")
CHIPS_COL = ("x", "yh")
ALL = ("z", "yl", "x", "yh", "c")
CHIPS = ("z", "yl", "x", "yh")
HIGH = lax.Precision.HIGH

SWAP = [(0, 1), (1, 0)]
TO_COLUMN = [(g * 16 + j, (j // 2) * 16 + 2 * g + j % 2) for g in range(8) for j in range(16)]
TO_OWNER = [(r * 16 + 2 * g + h, g * 16 + 8 * h + r) for r in range(8) for g in range(8) for h in range(2)]


def dot(a, b):
    return jnp.dot(a, b, precision=HIGH, preferred_element_type=jnp.float32)


def invert_map(local_map, count):
    positions = jnp.arange(count, dtype=jnp.int32)
    return jnp.sum(
        jnp.where(local_map[None, :] == positions[:, None], positions[None, :], 0), axis=1
    )


def spread(value, axes, count):
    copies = jnp.broadcast_to(value[None], (count,) + value.shape)
    return lax.all_to_all(copies, axes, 0, 0, tiled=True)


def shards(factor_panel, pivot_inverse, ancestor_inverse, diag_inverse, block_map):
    width = factor_panel.shape[1]
    core = lax.axis_index("c")
    my_row = lax.axis_index(ROW)
    group = lax.axis_index(CHIPS_COL)

    normed = dot(factor_panel, pivot_inverse)
    column_block = lax.ppermute(normed, ALL, TO_COLUMN)
    mine = spread(column_block, ROW, 8)
    other = lax.ppermute(mine, "c", SWAP)
    sources = jnp.concatenate([mine, other], axis=0)

    source = invert_map(block_map, block_map.shape[0])
    picks = lax.dynamic_slice_in_dim(source, group * 16 + core * 8, 8) - group * 16
    slots = picks // 2 + 8 * (picks % 2 != core)
    anc_blocks = jnp.take(sources, slots, axis=0)
    anc_cols = anc_blocks.reshape(8 * BLOCK, width)
    own_panel = lax.ppermute(
        lax.dynamic_index_in_dim(anc_blocks, my_row, 0, keepdims=False), ALL, TO_OWNER
    )

    partial_value = dot(ancestor_inverse, anc_cols).reshape(8, 2, BLOCK, width)
    keep = lax.dynamic_index_in_dim(partial_value, core, 1, keepdims=False)
    give = lax.dynamic_index_in_dim(partial_value, 1 - core, 1, keepdims=False)
    chip_sum = keep + lax.ppermute(give, "c", SWAP)
    parts = lax.all_to_all(chip_sum, CHIPS_COL, 0, 0, tiled=True)
    offdiag_block = -jnp.sum(parts, axis=0)

    term = lax.dot_general(
        own_panel,
        offdiag_block,
        (((0,), (0,)), ((), ())),
        precision=HIGH,
        preferred_element_type=jnp.float32,
    )
    half = width // 2
    keep_term = lax.dynamic_slice_in_dim(term, core * half, half, 0)
    give_term = lax.dynamic_slice_in_dim(term, (1 - core) * half, half, 0)
    term = keep_term + lax.ppermute(give_term, "c", SWAP)
    pieces = lax.all_to_all(term.reshape(64, half // 64, width), CHIPS, 0, 0, tiled=True)
    piece = jnp.sum(pieces, axis=0)
    mine_half = spread(piece, CHIPS, 64).reshape(half, width)
    other_half = lax.ppermute(mine_half, "c", SWAP)
    low = jnp.where(core == 0, mine_half, other_half)
    high = jnp.where(core == 0, other_half, mine_half)
    diag_block = diag_inverse - jnp.concatenate([low, high], axis=0)
    return (offdiag_block, diag_block)


def solution(mesh):
    fine = Mesh(mesh.devices.reshape(4, 2, 4, 2, 2), ALL)
    rows, cols = ROW, ("x", "yh", "c")
    placed = (P(ALL, None), P(), P(rows, cols), P(), P())
    return jax.shard_map(
        shards,
        mesh=fine,
        in_specs=placed,
        out_specs=(P(ALL, None), P()),
        check_vma=False,
    )
```

```python
import jax
import jax.numpy as jnp
from jax import lax
from jax.experimental import pallas as pl
from jax.experimental.pallas import tpu as pltpu
from jax.sharding import Mesh, PartitionSpec as P

BLOCK = 128
ROW = ("z", "yl")
CHIPS_COL = ("x", "yh")
ALL = ("z", "yl", "x", "yh", "c")
CHIPS = ("z", "yl", "x", "yh")
HIGH = lax.Precision.HIGH
SWAP = [(0, 1), (1, 0)]
TILE = 2


def flat(z, yl, x, yh, c):
    return (z * 2 + yl) * 16 + x * 4 + yh * 2 + c


DEVICES = [
    (z, yl, x, yh, c)
    for z in range(4)
    for yl in range(2)
    for x in range(4)
    for yh in range(2)
    for c in range(2)
]
TO_COLUMN = [
    (flat(z, yl, x, yh, c), flat(x, yh ^ (x & 1), z, yl, c)) for z, yl, x, yh, c in DEVICES
]
TO_OWNER = [
    (flat(z, yl, x, yh, c), flat(x, yh, 2 * c + (z >> 1), yl ^ (z & 1), z & 1))
    for z, yl, x, yh, c in DEVICES
]


def dot(a, b):
    return jnp.dot(a, b, precision=HIGH, preferred_element_type=jnp.float32)


def invert_map(local_map, count):
    positions = jnp.arange(count, dtype=jnp.int32)
    return jnp.sum(
        jnp.where(local_map[None, :] == positions[:, None], positions[None, :], 0), axis=1
    )


def spread(value, axes, count):
    copies = jnp.broadcast_to(value[None], (count,) + value.shape)
    return lax.all_to_all(copies, axes, 0, 0, tiled=True)


def split(value):
    high = value.astype(jnp.bfloat16)
    low = (value - high.astype(jnp.float32)).astype(jnp.bfloat16)
    return high, low


def half_kernel(table, a_ref, mine_ref, other_ref, out_ref, high_ref, low_ref):
    @pl.when(pl.program_id(0) == 0)
    def _():
        for t in range(8):
            slot = table[t]
            own = mine_ref[slot & 7]
            far = other_ref[slot & 7]
            high, low = split(jnp.where(slot < 8, own, far))
            high_ref[pl.ds(t * BLOCK, BLOCK), :] = high
            low_ref[pl.ds(t * BLOCK, BLOCK), :] = low

    rows = TILE * BLOCK
    a_high, a_low = split(a_ref[...].reshape(rows, a_ref.shape[-1]))
    total = jnp.dot(a_high, low_ref[...], preferred_element_type=jnp.float32)
    total += jnp.dot(a_low, high_ref[...], preferred_element_type=jnp.float32)
    total += jnp.dot(a_high, high_ref[...], preferred_element_type=jnp.float32)
    out_ref[...] = total.reshape(out_ref.shape)


def half_product(table, ancestor, mine, other):
    depth = ancestor.shape[-1]
    width = mine.shape[-1]
    whole = pl.BlockSpec((8, BLOCK, width), lambda i, table: (0, 0, 0))
    return pl.pallas_call(
        half_kernel,
        grid_spec=pltpu.PrefetchScalarGridSpec(
            num_scalar_prefetch=1,
            grid=(8 // TILE,),
            in_specs=[
                pl.BlockSpec((TILE, 1, BLOCK, depth), lambda i, table: (i, table[8], 0, 0)),
                whole,
                whole,
            ],
            out_specs=pl.BlockSpec((TILE, BLOCK, width), lambda i, table: (i, 0, 0)),
            scratch_shapes=[
                pltpu.VMEM((depth, width), jnp.bfloat16),
                pltpu.VMEM((depth, width), jnp.bfloat16),
            ],
        ),
        out_shape=jax.ShapeDtypeStruct((8, BLOCK, width), jnp.float32),
        cost_estimate=pl.CostEstimate(
            flops=3 * 2 * 8 * BLOCK * depth * width,
            bytes_accessed=4 * (8 * BLOCK * depth + 3 * 8 * BLOCK * width),
            transcendentals=0,
        ),
    )(table, ancestor, mine, other)


def shards(factor_panel, pivot_inverse, ancestor_inverse, diag_inverse, block_map):
    width = factor_panel.shape[1]
    core = lax.axis_index("c")
    z, yl = lax.axis_index("z"), lax.axis_index("yl")
    group = lax.axis_index(CHIPS_COL)

    normed = dot(factor_panel, pivot_inverse)
    column_block = lax.ppermute(normed, ALL, TO_COLUMN)
    mine = spread(column_block, ROW, 8).reshape(8, BLOCK, width)
    other = lax.ppermute(mine, "c", SWAP)

    source = invert_map(block_map, block_map.shape[0])
    picks = lax.dynamic_slice_in_dim(source, group * 16 + core * 8, 8) - group * 16
    slots = 2 * (picks >> 2) + (((picks >> 1) ^ (picks >> 2)) & 1)
    slots = slots + 8 * ((picks & 1) != core)
    send = (z >> 1) * 4 + (yl ^ (z & 1)) * 2 + (z & 1)
    slot = lax.dynamic_index_in_dim(slots, send, 0, keepdims=False)
    own_panel = jnp.where(
        slot < 8,
        lax.dynamic_index_in_dim(mine, slot & 7, 0, keepdims=False),
        lax.dynamic_index_in_dim(other, slot & 7, 0, keepdims=False),
    )
    own_panel = lax.ppermute(own_panel, ALL, TO_OWNER)

    ancestor = ancestor_inverse.reshape(8, 2, BLOCK, ancestor_inverse.shape[1])
    tables = [jnp.concatenate([slots, c[None]]).astype(jnp.int32) for c in (1 - core, core)]
    give = half_product(tables[0], ancestor, mine, other)
    keep = half_product(tables[1], ancestor, mine, other)
    chip_sum = keep + lax.ppermute(give, "c", SWAP)
    parts = lax.all_to_all(chip_sum, CHIPS_COL, 0, 0, tiled=True)
    offdiag_block = -jnp.sum(parts, axis=0)

    term = lax.dot_general(
        own_panel,
        offdiag_block,
        (((0,), (0,)), ((), ())),
        precision=HIGH,
        preferred_element_type=jnp.float32,
    )
    half = width // 2
    keep_term = lax.dynamic_slice_in_dim(term, core * half, half, 0)
    give_term = lax.dynamic_slice_in_dim(term, (1 - core) * half, half, 0)
    term = keep_term + lax.ppermute(give_term, "c", SWAP)
    rows = half // 64
    pieces = lax.all_to_all(term.reshape(64, rows, width), CHIPS, 0, 0, tiled=True)
    first = core * half + lax.axis_index(CHIPS) * rows
    piece = lax.dynamic_slice_in_dim(diag_inverse, first, rows, 0) - jnp.sum(pieces, axis=0)
    mine_half = spread(piece, CHIPS, 64).reshape(half, width)
    other_half = lax.ppermute(mine_half, "c", SWAP)
    low = jnp.where(core == 0, mine_half, other_half)
    high = jnp.where(core == 0, other_half, mine_half)
    return (offdiag_block, jnp.concatenate([low, high], axis=0))


def solution(mesh):
    fine = Mesh(mesh.devices.reshape(4, 2, 4, 2, 2), ALL)
    rows, cols = ROW, ("x", "yh", "c")
    placed = (P(ALL, None), P(), P(rows, cols), P(), P())
    return jax.shard_map(
        shards,
        mesh=fine,
        in_specs=placed,
        out_specs=(P(ALL, None), P()),
        check_vma=False,
    )
```

```python
import jax
import jax.numpy as jnp
from jax import lax
from jax.experimental import pallas as pl
from jax.experimental.pallas import tpu as pltpu
from jax.sharding import Mesh, PartitionSpec as P

BLOCK = 128
ROW = ("z", "yl")
CHIPS_COL = ("x", "yh")
ALL = ("z", "yl", "x", "yh", "c")
CHIPS = ("z", "yl", "x", "yh")
HIGH = lax.Precision.HIGH
SWAP = [(0, 1), (1, 0)]
TILE = 2
VMEM_LIMIT = 24 * 1024 * 1024


def flat(z, yl, x, yh, c):
    return (z * 2 + yl) * 16 + x * 4 + yh * 2 + c


DEVICES = [
    (z, yl, x, yh, c)
    for z in range(4)
    for yl in range(2)
    for x in range(4)
    for yh in range(2)
    for c in range(2)
]
TO_COLUMN = [
    (flat(z, yl, x, yh, c), flat(x, yh ^ (x & 1), z, yl, c)) for z, yl, x, yh, c in DEVICES
]
TO_OWNER = [
    (flat(z, yl, x, yh, c), flat(x, yh, 2 * c + (z >> 1), yl ^ (z & 1), z & 1))
    for z, yl, x, yh, c in DEVICES
]


def dot(a, b):
    return jnp.dot(a, b, precision=HIGH, preferred_element_type=jnp.float32)


def spread(value, axes, count):
    copies = jnp.broadcast_to(value[None], (count,) + value.shape)
    return lax.all_to_all(copies, axes, 0, 0, tiled=True)


def split(value):
    high = value.astype(jnp.bfloat16)
    low = (value - high.astype(jnp.float32)).astype(jnp.bfloat16)
    return high, low


def whole_call(kernel, inputs, outputs, scratch=()):
    whole = pl.BlockSpec(memory_space=pltpu.VMEM)
    table, *arrays = inputs
    return pl.pallas_call(
        kernel,
        in_specs=[pl.BlockSpec(memory_space=pltpu.SMEM)] + [whole] * len(arrays),
        out_specs=[whole] * len(outputs),
        out_shape=outputs,
        scratch_shapes=scratch,
        compiler_params=pltpu.CompilerParams(vmem_limit_bytes=VMEM_LIMIT),
        cost_estimate=pl.CostEstimate(flops=4096, bytes_accessed=4096, transcendentals=0),
    )(table, *arrays)


def prepare_kernel(table, mine_ref, other_ref, high_ref, low_ref, own_ref):
    for s in range(16):
        source = mine_ref.at[s] if s < 8 else other_ref.at[s - 8]
        place = table[s]

        @pl.when((place >= 0) & (place < 8))
        def _():
            value = source[...]
            rows = pl.ds(pl.multiple_of(place * BLOCK, BLOCK), BLOCK)
            high, low = split(value)
            high_ref[rows, :] = high
            low_ref[rows, :] = low

            @pl.when(place == table[16])
            def _():
                own_ref[...] = value


def combine_kernel(table, keep_ref, taken_ref, out):
    out[...] = keep_ref[...] + taken_ref[...]


def total_kernel(table, parts, out, given, kept):
    value = parts[0]
    for k in range(1, 8):
        value = value + parts[k]
    value = -value
    half = value.shape[1] // 2
    out[...] = value
    first_core = table[17] == 0
    given[...] = jnp.where(first_core, value[:, half:], value[:, :half])
    kept[...] = jnp.where(first_core, value[:, :half], value[:, half:])


def assemble_kernel(table, mine, other, out):
    half = mine.shape[1]
    first_core = table[17] == 0
    out[:, :half] = jnp.where(first_core, mine[...], other[...])
    out[:, half:] = jnp.where(first_core, other[...], mine[...])


def half_kernel(table, a_ref, high_ref, low_ref, out_ref):
    rows = TILE * BLOCK
    a_high, a_low = split(a_ref[...].reshape(rows, a_ref.shape[-1]))
    total = jnp.dot(a_high, low_ref[...], preferred_element_type=jnp.float32)
    total += jnp.dot(a_low, high_ref[...], preferred_element_type=jnp.float32)
    total += jnp.dot(a_high, high_ref[...], preferred_element_type=jnp.float32)
    out_ref[...] = total.reshape(out_ref.shape)


def half_product(table, ancestor, high, low):
    depth, width = high.shape
    whole = pl.BlockSpec(memory_space=pltpu.VMEM)
    return pl.pallas_call(
        half_kernel,
        grid_spec=pltpu.PrefetchScalarGridSpec(
            num_scalar_prefetch=1,
            grid=(8 // TILE,),
            in_specs=[
                pl.BlockSpec((TILE, 1, BLOCK, depth), lambda i, table: (i, table[0], 0, 0)),
                whole,
                whole,
            ],
            out_specs=pl.BlockSpec((TILE, BLOCK, width), lambda i, table: (i, 0, 0)),
        ),
        out_shape=jax.ShapeDtypeStruct((8, BLOCK, width), jnp.float32),
        compiler_params=pltpu.CompilerParams(vmem_limit_bytes=VMEM_LIMIT),
        cost_estimate=pl.CostEstimate(
            flops=3 * 2 * 8 * BLOCK * depth * width,
            bytes_accessed=4 * (8 * BLOCK * depth + 2 * 8 * BLOCK * width),
            transcendentals=0,
        ),
    )(table, ancestor, high, low)


def shards(factor_panel, pivot_inverse, ancestor_inverse, diag_inverse, block_map):
    width = factor_panel.shape[1]
    core = lax.axis_index("c")
    z, yl = lax.axis_index("z"), lax.axis_index("yl")
    group = lax.axis_index(CHIPS_COL)

    half = width // 2
    first = lax.axis_index(CHIPS) * (width // 64)
    diag_piece = lax.dynamic_slice(diag_inverse, (first, core * half), (width // 64, half))
    half = width // 2
    first = lax.axis_index(CHIPS) * (width // 64)
    diag_piece = lax.dynamic_slice(diag_inverse, (first, core * half), (width // 64, half))
    row = jnp.arange(8, dtype=jnp.int32)
    columns = 2 * (row >> 1) + (row ^ (row >> 1)) % 2
    columns = jnp.concatenate([columns * 2 + core, columns * 2 + 1 - core])
    in_group = lax.dynamic_slice_in_dim(block_map, group * 16, 16) - group * 16
    chosen = columns[:, None] == jnp.arange(16, dtype=jnp.int32)[None, :]
    places = jnp.sum(jnp.where(chosen, in_group[None, :], 0), axis=1) - 8 * core
    send = (z >> 1) * 4 + (yl ^ (z & 1)) * 2 + (z & 1)
    places = jnp.concatenate([places, send[None], core[None]]).astype(jnp.int32)
    tables = [c[None].astype(jnp.int32) for c in (1 - core, core)]
    ancestor = ancestor_inverse.reshape(8, 2, BLOCK, ancestor_inverse.shape[1])
    ancestor = pltpu.with_memory_space_constraint(ancestor, pltpu.HBM)
    block = jax.ShapeDtypeStruct(factor_panel.shape, jnp.float32)
    blocks = jax.ShapeDtypeStruct((8,) + factor_panel.shape, jnp.float32)
    half_panel = jax.ShapeDtypeStruct((8 * BLOCK, width), jnp.bfloat16)

    moved = lax.ppermute(factor_panel, ALL, TO_COLUMN)
    column_block = dot(moved, pivot_inverse)
    column_block, places, tables, diag_piece = lax.optimization_barrier(
        (column_block, places, tables, diag_piece)
    )
    mine = spread(column_block, ROW, 8).reshape(8, BLOCK, width)
    other = lax.ppermute(mine, "c", SWAP)
    high, low, own = whole_call(
        prepare_kernel, [places, mine, other], [half_panel, half_panel, block]
    )
    own_panel = lax.ppermute(own, ALL, TO_OWNER)
    give = half_product(tables[0], ancestor, high, low)
    taken = lax.ppermute(give, "c", SWAP)
    keep = half_product(tables[1], ancestor, high, low)
    (chip_sum,) = whole_call(combine_kernel, [places, keep, taken], [blocks])
    chip_sum, own_panel = lax.optimization_barrier((chip_sum, own_panel))
    parts = lax.all_to_all(chip_sum, CHIPS_COL, 0, 0, tiled=True)
    columns = jax.ShapeDtypeStruct((BLOCK, half), jnp.float32)
    offdiag_block, given, kept = whole_call(
        total_kernel, [places, parts], [block, columns, columns]
    )

    def term(value):
        return lax.dot_general(
            own_panel,
            value,
            (((0,), (0,)), ((), ())),
            precision=HIGH,
            preferred_element_type=jnp.float32,
        )

    summed = lax.ppermute(term(given), "c", SWAP) + term(kept)
    summed, offdiag_block = lax.optimization_barrier((summed, offdiag_block))
    pieces = lax.all_to_all(summed.reshape(64, width // 64, half), CHIPS, 0, 0, tiled=True)
    mine_half = spread(diag_piece - jnp.sum(pieces, axis=0), CHIPS, 64).reshape(width, half)
    other_half = lax.ppermute(mine_half, "c", SWAP)
    (diag_block,) = whole_call(
        assemble_kernel,
        [places, mine_half, other_half],
        [jax.ShapeDtypeStruct(diag_inverse.shape, jnp.float32)],
    )
    return (offdiag_block, diag_block)


def solution(mesh):
    fine = Mesh(mesh.devices.reshape(4, 2, 4, 2, 2), ALL)
    rows, cols = ROW, ("x", "yh", "c")
    placed = (P(ALL, None), P(), P(rows, cols), P(), P())

    return jax.shard_map(
        shards,
        mesh=fine,
        in_specs=placed,
        out_specs=(P(ALL, None), P()),
        check_vma=False,
    )
```

```python
import jax
import jax.numpy as jnp
from jax import lax
from jax.experimental import pallas as pl
from jax.experimental.pallas import tpu as pltpu
from jax.sharding import Mesh, PartitionSpec as P

BLOCK = 128
ROW = ("z", "yl")
CHIPS_COL = ("x", "yh")
ALL = ("z", "yl", "x", "yh", "c")
CHIPS = ("z", "yl", "x", "yh")
SWAP = [(0, 1), (1, 0)]
TILE = 2
VMEM_LIMIT = 24 * 1024 * 1024


def flat(z, yl, x, yh, c):
    return (z * 2 + yl) * 16 + x * 4 + yh * 2 + c


DEVICES = [
    (z, yl, x, yh, c)
    for z in range(4)
    for yl in range(2)
    for x in range(4)
    for yh in range(2)
    for c in range(2)
]
TO_COLUMN = [
    (flat(z, yl, x, yh, c), flat((z - x) % 4, yh ^ (x >> 1), z, yl, c))
    for z, yl, x, yh, c in DEVICES
]


def turn(k):
    return [(i, (i + k) % 4) for i in range(4)]


def split(value):
    high = value.astype(jnp.bfloat16)
    low = (value - high.astype(jnp.float32)).astype(jnp.bfloat16)
    return high, low


def whole_call(kernel, inputs, outputs, scratch=()):
    whole = pl.BlockSpec(memory_space=pltpu.VMEM)
    table, *arrays = inputs
    return pl.pallas_call(
        kernel,
        in_specs=[pl.BlockSpec(memory_space=pltpu.SMEM)] + [whole] * len(arrays),
        out_specs=[whole] * len(outputs),
        out_shape=outputs,
        scratch_shapes=scratch,
        compiler_params=pltpu.CompilerParams(vmem_limit_bytes=VMEM_LIMIT),
        cost_estimate=pl.CostEstimate(flops=4096, bytes_accessed=4096, transcendentals=0),
    )(table, *arrays)


def prepare_kernel(table, mine_ref, other_ref, high_ref, low_ref):
    for s in range(16):
        source = mine_ref.at[s] if s < 8 else other_ref.at[s - 8]
        place = table[s]

        @pl.when((place >= 0) & (place < 8))
        def _():
            rows = pl.ds(pl.multiple_of(place * BLOCK, BLOCK), BLOCK)
            high, low = split(source[...])
            high_ref[rows, :] = high
            low_ref[rows, :] = low


def order_kernel(table, mine_ref, other_ref, high_ref, low_ref):
    for s in range(16):
        source = mine_ref.at[s] if s < 8 else other_ref.at[s - 8]
        place = table[s]

        @pl.when((place & 1) == table[16])
        def _():
            lanes = pl.ds(pl.multiple_of((place >> 1) * BLOCK, BLOCK), BLOCK)
            high, low = split(source[...].T)
            high_ref[:, lanes] = high
            low_ref[:, lanes] = low


def product(left_high, left_low, value):
    high, low = split(value)
    total = jnp.dot(left_high, low, preferred_element_type=jnp.float32)
    total += jnp.dot(left_low, high, preferred_element_type=jnp.float32)
    total += jnp.dot(left_high, high, preferred_element_type=jnp.float32)
    return total


def given_kernel(table, high_ref, low_ref, value_ref, out):
    value = value_ref[...].reshape(8 * BLOCK, value_ref.shape[2])
    out[...] = product(high_ref[...], low_ref[...], value)


def kept_kernel(table, high_ref, low_ref, value_ref, taken_ref, out):
    value = value_ref[...].reshape(8 * BLOCK, value_ref.shape[2])
    total = product(high_ref[...], low_ref[...], value) + taken_ref[...]
    out[...] = total.reshape(out.shape)


def piece_kernel(table, base, pieces, out):
    value = base[...]
    for k in range(64):
        value = value + pieces[k]
    for k in range(64):
        out[k] = value


def norm_kernel(table, moved, pivot, out):
    out[...] = jnp.dot(
        moved[...],
        pivot[...],
        precision=lax.Precision.HIGHEST,
        preferred_element_type=jnp.float32,
    )


def spread_kernel(table, moved, pivot, out):
    value = jnp.dot(
        moved[...],
        pivot[...],
        precision=lax.Precision.HIGHEST,
        preferred_element_type=jnp.float32,
    )
    for k in range(8):
        out[k] = value


def pair_kernel(table, first, second, out):
    out[0] = first[...]
    out[1] = second[...]


def stack_kernel(table, *refs):
    for k in range(4):
        refs[4][2 * k : 2 * k + 2] = refs[k][...]


def combine_kernel(table, keep_ref, taken_ref, given, kept, *outs):
    half = given.shape[2]
    first_core = table[16] == 0
    for k in range(4):
        for y in range(2):
            i = ((table[17] + k) & 3) * 2 + y
            value = keep_ref[i] + taken_ref[i]
            outs[k][y] = value
            given[i] = jnp.where(first_core, value[:, half:], value[:, :half])
            kept[i] = jnp.where(first_core, value[:, :half], value[:, half:])


def line_kernel(table, own, first, second, third, keep, give):
    y = table[18]
    keep[...] = own[y] + first[y] + second[y] + third[y]
    give[...] = own[1 - y] + first[1 - y] + second[1 - y] + third[1 - y]


def total_kernel(table, keep, taken, out):
    out[...] = -(keep[...] + taken[...])


def assemble_kernel(table, mine, other, out):
    half = mine.shape[1]
    first_core = table[16] == 0
    out[:, :half] = jnp.where(first_core, mine[...], other[...])
    out[:, half:] = jnp.where(first_core, other[...], mine[...])


def half_kernel(table, a_ref, high_ref, low_ref, out_ref):
    rows = TILE * BLOCK

    @pl.loop(0, 8 // TILE)
    def _(i):
        tile = a_ref[pl.ds(i * TILE, TILE), table[0]]
        a_high, a_low = split(tile.reshape(rows, a_ref.shape[-1]))
        total = jnp.dot(a_high, low_ref[...], preferred_element_type=jnp.float32)
        total += jnp.dot(a_low, high_ref[...], preferred_element_type=jnp.float32)
        total += jnp.dot(a_high, high_ref[...], preferred_element_type=jnp.float32)
        out_ref[pl.ds(i * TILE, TILE)] = total.reshape(TILE, BLOCK, total.shape[-1])


def shards(factor_panel, pivot_inverse, ancestor_inverse, diag_inverse, block_map):
    width = factor_panel.shape[1]
    half = width // 2
    core = lax.axis_index("c")
    chip_row = lax.axis_index(ROW)
    group = lax.axis_index(CHIPS_COL)
    first = lax.axis_index(CHIPS) * (width // 64)
    diag_piece = lax.dynamic_slice(diag_inverse, (first, core * half), (width // 64, half))

    mine_at = jnp.stack([core, lax.axis_index("x"), lax.axis_index("yh")])

    def places(owner, chips, offset):
        columns = jnp.concatenate([chips * 2 + core, chips * 2 + 1 - core])
        in_group = lax.dynamic_slice_in_dim(block_map, owner * 16, 16) - owner * 16
        chosen = columns[:, None] == jnp.arange(16, dtype=jnp.int32)[None, :]
        found = jnp.sum(jnp.where(chosen, in_group[None, :], 0), axis=1) - offset
        return jnp.concatenate([found, mine_at]).astype(jnp.int32)

    row = jnp.arange(8, dtype=jnp.int32)
    x = (lax.axis_index("x") - (row >> 1)) & 3
    column_places = places(group, 2 * x + ((row ^ (x >> 1)) & 1), 8 * core)
    reach = (lax.axis_index("x") - (row >> 1)) & 3
    row_places = places(chip_row, 2 * reach + ((row & 1) ^ lax.axis_index("yh")), 0)
    tables = [c[None].astype(jnp.int32) for c in (1 - core, core)]
    ancestor = ancestor_inverse.reshape(8, 2, BLOCK, ancestor_inverse.shape[1])
    ancestor = pltpu.with_memory_space_constraint(ancestor, pltpu.VMEM)
    block = jax.ShapeDtypeStruct(factor_panel.shape, jnp.float32)
    blocks = jax.ShapeDtypeStruct((8,) + factor_panel.shape, jnp.float32)
    half_blocks = jax.ShapeDtypeStruct((8, BLOCK, half), jnp.float32)
    half_panel = jax.ShapeDtypeStruct((8 * BLOCK, width), jnp.bfloat16)

    moved = lax.ppermute(factor_panel, ALL, TO_COLUMN)
    panel, pivot_inverse, column_places, row_places, tables, diag_piece = (
        lax.optimization_barrier(
            (factor_panel, pivot_inverse, column_places, row_places, tables, diag_piece)
        )
    )
    pair = jax.ShapeDtypeStruct((2, BLOCK, width), jnp.float32)
    (normed,) = whole_call(norm_kernel, [row_places, panel, pivot_inverse], [block])
    beside = lax.ppermute(normed, "yh", SWAP)
    row_lines = list(whole_call(pair_kernel, [row_places, normed, beside], [pair]))
    for k in range(1, 4):
        row_lines.append(lax.ppermute(row_lines[0], "x", turn(k)))
    moved, ancestor = lax.optimization_barrier((moved, ancestor))
    (copies,) = whole_call(spread_kernel, [column_places, moved, pivot_inverse], [blocks])
    mine = lax.all_to_all(copies, ROW, 0, 0, tiled=True)
    other = lax.ppermute(mine, "c", SWAP)
    high, low = whole_call(prepare_kernel, [column_places, mine, other], [half_panel, half_panel])
    (row_mine,) = whole_call(stack_kernel, [row_places, *row_lines], [blocks])
    row_other = lax.ppermute(row_mine, "c", SWAP)
    turned = jax.ShapeDtypeStruct((width, 8 * BLOCK), jnp.bfloat16)
    row_high, row_low = whole_call(
        order_kernel, [row_places, row_mine, row_other], [turned, turned]
    )
    (give,) = whole_call(half_kernel, [tables[0], ancestor, high, low], [blocks])
    taken = lax.ppermute(give, "c", SWAP)
    (keep,) = whole_call(half_kernel, [tables[1], ancestor, high, low], [blocks])
    given, kept, *lines = whole_call(
        combine_kernel, [row_places, keep, taken], [half_blocks, half_blocks] + [pair] * 4
    )
    (given,) = whole_call(
        given_kernel,
        [row_places, row_high, row_low, given],
        [jax.ShapeDtypeStruct((width, half), jnp.float32)],
    )
    given = lax.ppermute(given, "c", SWAP)
    for k in range(1, 4):
        lines[k] = lax.ppermute(lines[k], "x", turn(k))
    slabs = jax.ShapeDtypeStruct((64, width // 64, half), jnp.float32)
    (summed,) = whole_call(
        kept_kernel, [row_places, row_high, row_low, kept, given], [slabs]
    )
    pieces = lax.all_to_all(summed, CHIPS, 0, 0, tiled=True)
    (copies,) = whole_call(piece_kernel, [row_places, diag_piece, pieces], [slabs])
    keep_line, give_line = whole_call(line_kernel, [row_places, *lines], [block, block])
    take_line = lax.ppermute(give_line, "yh", SWAP)
    mine_half = lax.all_to_all(copies, CHIPS, 0, 0, tiled=True).reshape(width, half)
    other_half = lax.ppermute(mine_half, "c", SWAP)
    (offdiag_block,) = whole_call(total_kernel, [row_places, keep_line, take_line], [block])
    (diag_block,) = whole_call(
        assemble_kernel,
        [row_places, mine_half, other_half],
        [jax.ShapeDtypeStruct(diag_inverse.shape, jnp.float32)],
    )
    return (offdiag_block, diag_block)


def solution(mesh):
    fine = Mesh(mesh.devices.reshape(4, 2, 4, 2, 2), ALL)
    rows, cols = ROW, ("x", "yh", "c")
    placed = (P(ALL, None), P(), P(rows, cols), P(), P())

    return jax.shard_map(
        shards,
        mesh=fine,
        in_specs=placed,
        out_specs=(P(ALL, None), P()),
        check_vma=False,
    )
```
